32 devices in a mesh: crop: 4 (over x, core), row: 8 (over z, y).
Axes of the slice: x: 2, y: 2, z: 4, core: 2. Of those that a mesh axis runs over, the one named last changes fastest.
Arguments:
- pair: bfloat16 [4, 64, 64, 128], P('crop', 'row'), may hold values from -6 to 6
- cotangent: bfloat16 [4, 64, 64, 128], P('crop', 'row'), may hold values from -6 to 6
- lengths: int32 [4], P('crop'), may hold values from 32 to 64
- proj_weight: bfloat16 [128, 640], replicated, may hold values from -0.5 to 0.5
- out_weight: bfloat16 [128, 128], replicated, may hold values from -0.5 to 0.5
- up_weight: bfloat16 [128, 512], replicated, may hold values from -0.5 to 0.5
- down_weight: bfloat16 [512, 128], replicated, may hold values from -0.25 to 0.25
- norm_gain: float32 [3, 128], replicated, may hold values from 0.1 to 1.9
- norm_bias: float32 [3, 128], replicated, may hold values from -3 to 3
Outputs:
- grad_pair: bfloat16 [4, 64, 64, 128], P('crop', 'row')
- grad_proj: float32 [128, 640], replicated
- grad_out: float32 [128, 128], replicated
- grad_up: float32 [128, 512], replicated
- grad_down: float32 [512, 128], replicated
- grad_gain: float32 [3, 128], replicated
- grad_bias: float32 [3, 128], replicated
The draws below stay inside these ranges and needn't reach their ends.
Inputs may be any that keep to these rules, and one draw needn't show every extreme that they name: lengths[s] residues of crop s are present; the rest are masked.
All inputs are finite; a program needn't handle non-finite values.
Results may differ from the reference program's by a relative error of at most 0.009.
Values may be sent and summed in bfloat16 or wider, within the bound.
No kernel may reach another device: no remote copies, remote signals or barrier semaphores. Data moves between devices by JAX's collectives and lax.ppermute only.
A program may use at most 128 MiB of HBM per device.

```python
import jax
import jax.numpy as jnp
from jax import lax

CH = 128
HID = 512
L = 64
CROPS = 4


def set_ends(drawn, stream_key, smallest, largest):
    longest = drawn.shape.index(max(drawn.shape))
    spots = []
    for shift in (0, 1):
        where = [jax.random.randint(jax.random.fold_in(stream_key, axis), (), 0, length) for axis, length in enumerate(drawn.shape)]
        where[longest] = (where[longest] + shift) % drawn.shape[longest]
        spots.append(tuple(where))
    return drawn.at[spots[0]].set(smallest).at[spots[1]].set(largest)


def block_scale(stream_key, extent, pieces, low, top_value):
    loudness = 1.0
    for dim, shards_of in pieces:
        steps = jax.random.uniform(jax.random.fold_in(jax.random.fold_in(stream_key, 6), dim), (shards_of,), jnp.float32, low / len(pieces), top_value / len(pieces))
        loudness = loudness * jnp.repeat(jnp.exp(steps), extent[dim] // shards_of).reshape((-1,) + (1,) * (len(extent) - 1 - dim))
    return loudness


def gaussian(rng, shape, width, most, pieces=(), kind=jnp.bfloat16):
    level = block_scale(rng, shape, pieces, -0.22, 0.18) if pieces else 1.0
    values = jax.random.normal(rng, shape, jnp.float32) * width * level
    return jnp.minimum(jnp.maximum(values, -most), most).astype(kind)


def setup_inputs(seed: int = 0) -> dict:
    streams_of = jax.random.split(jax.random.key(seed), 10)
    pair = gaussian(streams_of[0], (CROPS, L, L, CH), 1.0, 6.0, ((0, 4), (1, 8)))
    cotangent = gaussian(streams_of[1], (CROPS, L, L, CH), 1.0, 6.0, ((0, 4), (1, 8)))
    lengths = set_ends(jax.random.randint(streams_of[2], (CROPS,), L // 2, L + 1), jax.random.fold_in(streams_of[2], 1), L // 2, L).astype(jnp.int32)
    proj_weight = gaussian(streams_of[3], (CH, 5 * CH), CH ** -0.5, 0.5)
    out_weight = gaussian(streams_of[4], (CH, CH), CH ** -0.5, 0.5)
    up_weight = gaussian(streams_of[5], (CH, HID), CH ** -0.5, 0.5)
    down_weight = gaussian(streams_of[6], (HID, CH), HID ** -0.5, 0.25)
    norm_gain = jnp.clip(1.0 + 0.18 * jax.random.normal(streams_of[7], (3, CH), jnp.float32), 0.1, 1.9)
    norm_bias = gaussian(streams_of[8], (3, CH), 0.5, 3.0, (), jnp.float32)
    return dict(pair=pair, cotangent=cotangent, lengths=lengths, proj_weight=proj_weight, out_weight=out_weight, up_weight=up_weight, down_weight=down_weight, norm_gain=norm_gain, norm_bias=norm_bias)


EPSILON = 1e-05

def contract(pattern, left_side, right_side):
    return jnp.einsum(pattern, left_side.astype(jnp.float32), right_side.astype(jnp.float32))

def norm_forward(values, gain_vec, bias_vec, norm_axis):
    center = values - lax.optimization_barrier(jnp.mean(values, axis=norm_axis, keepdims=True))
    inv_std = lax.rsqrt(lax.optimization_barrier(jnp.mean(center * center, axis=norm_axis, keepdims=True)) + EPSILON)
    normed = center * inv_std
    return (normed, inv_std, normed * gain_vec + bias_vec)

def norm_backward(upstream, normed, inv_std, gain_vec, norm_axis, others):
    grad_gain = lax.optimization_barrier(jnp.sum(upstream * normed, axis=others))
    grad_bias = lax.optimization_barrier(jnp.sum(upstream, axis=others))
    scaled = upstream * gain_vec
    result = inv_std * (scaled - lax.optimization_barrier(jnp.mean(scaled, axis=norm_axis, keepdims=True)) - normed * lax.optimization_barrier(jnp.mean(scaled * normed, axis=norm_axis, keepdims=True)))
    return (result, grad_gain, grad_bias)

def enter_rows(pair_rows, row_keep, col_keep, proj_weight, norm_gain, norm_bias):
    channels = pair_rows.shape[2]
    normed_in, inv_in, scaled_in = norm_forward(pair_rows.astype(jnp.float32), norm_gain[0], norm_bias[0], 2)
    input_bf = scaled_in.astype(jnp.bfloat16)
    factor_pre = contract('rld,de->erl', input_bf, proj_weight[:, :4 * channels])
    gate_pre = contract('rld,de->rle', input_bf, proj_weight[:, 4 * channels:])
    keep_both = row_keep[:, None] * col_keep[None, :]
    left_bf = (jax.nn.sigmoid(factor_pre[:channels]) * factor_pre[channels:2 * channels] * keep_both).astype(jnp.bfloat16)
    right_bf = (jax.nn.sigmoid(factor_pre[2 * channels:3 * channels]) * factor_pre[3 * channels:] * keep_both).astype(jnp.bfloat16)
    return (input_bf, normed_in, inv_in, factor_pre, gate_pre, keep_both, left_bf, right_bf)

def middle_rows(pair_rows, cot_rows, product_bf, gate_pre, out_weight, up_weight, down_weight, norm_gain, norm_bias):
    prod_normed, prod_inv, prod_scaled = norm_forward(product_bf.astype(jnp.float32), norm_gain[1][:, None, None], norm_bias[1][:, None, None], 0)
    prod_norm_bf = prod_scaled.astype(jnp.bfloat16)
    update = contract('crj,cd->rjd', prod_norm_bf, out_weight)
    gate_sig = jax.nn.sigmoid(gate_pre)
    first_bf = (pair_rows.astype(jnp.float32) + gate_sig * update).astype(jnp.bfloat16)
    tran_normed, tran_inv, tran_scaled = norm_forward(first_bf.astype(jnp.float32), norm_gain[2], norm_bias[2], 2)
    tran_bf = tran_scaled.astype(jnp.bfloat16)
    hidden_pre = contract('rld,dh->rlh', tran_bf, up_weight)
    hidden_sig = jax.nn.sigmoid(hidden_pre)
    hidden_bf = (hidden_pre * hidden_sig).astype(jnp.bfloat16)
    grad_down = contract('rlh,rld->hd', hidden_bf, cot_rows)
    hidden_grad_bf = (contract('rld,hd->rlh', cot_rows, down_weight) * hidden_sig * (1.0 + hidden_pre * (1.0 - hidden_sig))).astype(jnp.bfloat16)
    grad_up = contract('rld,rlh->dh', tran_bf, hidden_grad_bf)
    tran_grad = contract('rlh,dh->rld', hidden_grad_bf, up_weight)
    first_grad, gain_tran, bias_tran = norm_backward(tran_grad, tran_normed, tran_inv, norm_gain[2], 2, (0, 1))
    first_grad = first_grad + cot_rows.astype(jnp.float32)
    update_grad_bf = (first_grad * gate_sig).astype(jnp.bfloat16)
    gate_grad_bf = (first_grad * update * gate_sig * (1.0 - gate_sig)).astype(jnp.bfloat16)
    grad_out = contract('crj,rjd->cd', prod_norm_bf, update_grad_bf)
    norm_grad = contract('rjd,cd->crj', update_grad_bf, out_weight)
    prod_grad, gain_prod, bias_prod = norm_backward(norm_grad, prod_normed, prod_inv, norm_gain[1][:, None, None], 0, (1, 2))
    return (prod_grad.astype(jnp.bfloat16), first_grad, gate_grad_bf, grad_out, grad_up, grad_down, gain_prod, bias_prod, gain_tran, bias_tran)

def leave_rows(left_grad, right_grad, factor_pre, keep_both, gate_grad_bf, input_bf, normed_in, inv_in, first_grad, proj_weight, norm_gain):
    channels = gate_grad_bf.shape[2]
    sig_left = jax.nn.sigmoid(factor_pre[:channels])
    lin_left = factor_pre[channels:2 * channels]
    sig_right = jax.nn.sigmoid(factor_pre[2 * channels:3 * channels])
    lin_right = factor_pre[3 * channels:]
    masked_left = left_grad.astype(jnp.float32) * keep_both
    masked_right = right_grad.astype(jnp.float32) * keep_both
    factor_grad = jnp.concatenate([masked_left * lin_left * sig_left * (1.0 - sig_left), masked_left * sig_left, masked_right * lin_right * sig_right * (1.0 - sig_right), masked_right * sig_right], axis=0).astype(jnp.bfloat16)
    grad_proj = jnp.concatenate([contract('rld,erl->de', input_bf, factor_grad), contract('rld,rle->de', input_bf, gate_grad_bf)], axis=1)
    input_grad = contract('erl,de->rld', factor_grad, proj_weight[:, :4 * channels]) + contract('rle,de->rld', gate_grad_bf, proj_weight[:, 4 * channels:])
    pair_grad, gain_in, bias_in = norm_backward(input_grad, normed_in, inv_in, norm_gain[0], 2, (0, 1))
    return ((pair_grad + first_grad).astype(jnp.bfloat16), grad_proj, gain_in, bias_in)

def reference(pair, cotangent, lengths, proj_weight, out_weight, up_weight, down_weight, norm_gain, norm_bias):

    def one_crop(operands):
        pair_crop, cot_crop, length = operands
        row_keep = (jnp.arange(L, dtype=jnp.int32) < length).astype(jnp.float32)
        entered = enter_rows(pair_crop, row_keep, row_keep, proj_weight, norm_gain, norm_bias)
        input_bf, normed_in, inv_in, factor_pre, gate_pre, keep_both, left_bf, right_bf = entered
        product_bf = contract('cik,cjk->cij', left_bf, right_bf).astype(jnp.bfloat16)
        middle = middle_rows(pair_crop, cot_crop, product_bf, gate_pre, out_weight, up_weight, down_weight, norm_gain, norm_bias)
        prod_grad_bf, first_grad, gate_grad_bf, grad_out, grad_up, grad_down, gain_prod, bias_prod, gain_tran, bias_tran = middle
        left_grad = contract('cij,cjk->cik', prod_grad_bf, right_bf).astype(jnp.bfloat16)
        right_grad = contract('cij,cik->cjk', prod_grad_bf, left_bf).astype(jnp.bfloat16)
        pair_grad, grad_proj, gain_in, bias_in = leave_rows(left_grad, right_grad, factor_pre, keep_both, gate_grad_bf, input_bf, normed_in, inv_in, first_grad, proj_weight, norm_gain)
        return (pair_grad, grad_proj, grad_out, grad_up, grad_down, jnp.stack([gain_in, gain_prod, gain_tran]), jnp.stack([bias_in, bias_prod, bias_tran]))
    results = lax.map(one_crop, (pair, cotangent, lengths))
    factor = 1.0 / L
    return (results[0], lax.optimization_barrier(jnp.sum(results[1], axis=0)) * factor, lax.optimization_barrier(jnp.sum(results[2], axis=0)) * factor, lax.optimization_barrier(jnp.sum(results[3], axis=0)) * factor, lax.optimization_barrier(jnp.sum(results[4], axis=0)) * factor, lax.optimization_barrier(jnp.sum(results[5], axis=0)) * factor, lax.optimization_barrier(jnp.sum(results[6], axis=0)) * factor)
```

```python
import functools

import jax
import jax.numpy as jnp
from jax import lax
from jax.experimental import pallas as pl
from jax.experimental.pallas import tpu as pltpu
from jax.sharding import PartitionSpec as P

EPSILON = 1e-05


def for_sending(x):
    return jax.tree.map(lambda a: a.astype(jnp.bfloat16) if a.dtype == jnp.float32 else a, x)


def contract(pattern, left_side, right_side):
    return jnp.einsum(pattern, left_side, right_side, preferred_element_type=jnp.float32)


def norm_forward(values, gain_vec, bias_vec, norm_axis):
    center = values - jnp.mean(values, axis=norm_axis, keepdims=True)
    inv_std = lax.rsqrt(jnp.mean(center * center, axis=norm_axis, keepdims=True) + EPSILON)
    normed = center * inv_std
    return (normed, inv_std, normed * gain_vec + bias_vec)


def norm_backward(upstream, normed, inv_std, gain_vec, norm_axis, others):
    grad_gain = jnp.sum(upstream * normed, axis=others)
    grad_bias = jnp.sum(upstream, axis=others)
    scaled = upstream * gain_vec
    result = inv_std * (
        scaled
        - jnp.mean(scaled, axis=norm_axis, keepdims=True)
        - normed * jnp.mean(scaled * normed, axis=norm_axis, keepdims=True)
    )
    return (result, grad_gain, grad_bias)


def enter_rows(pair_rows, row_keep, col_keep, proj_weight, norm_gain, norm_bias):
    channels = pair_rows.shape[2]
    normed_in, inv_in, scaled_in = norm_forward(
        pair_rows.astype(jnp.float32), norm_gain[0], norm_bias[0], 2
    )
    input_bf = scaled_in.astype(jnp.bfloat16)
    factor_pre = contract("rld,de->erl", input_bf, proj_weight[:, : 4 * channels])
    gate_pre = contract("rld,de->rle", input_bf, proj_weight[:, 4 * channels :])
    keep_both = row_keep[:, None] * col_keep[None, :]
    left_bf = (
        jax.nn.sigmoid(factor_pre[:channels]) * factor_pre[channels : 2 * channels] * keep_both
    ).astype(jnp.bfloat16)
    right_bf = (
        jax.nn.sigmoid(factor_pre[2 * channels : 3 * channels])
        * factor_pre[3 * channels :]
        * keep_both
    ).astype(jnp.bfloat16)
    return (input_bf, normed_in, inv_in, factor_pre, gate_pre, keep_both, left_bf, right_bf)


def middle_rows(
    pair_rows,
    cot_rows,
    product_bf,
    gate_pre,
    out_weight,
    up_weight,
    down_weight,
    norm_gain,
    norm_bias,
):
    prod_normed, prod_inv, prod_scaled = norm_forward(
        product_bf.astype(jnp.float32), norm_gain[1][:, None, None], norm_bias[1][:, None, None], 0
    )
    prod_norm_bf = prod_scaled.astype(jnp.bfloat16)
    update = contract("crj,cd->rjd", prod_norm_bf, out_weight)
    gate_sig = jax.nn.sigmoid(gate_pre)
    first_bf = (pair_rows.astype(jnp.float32) + gate_sig * update).astype(jnp.bfloat16)
    tran_normed, tran_inv, tran_scaled = norm_forward(
        first_bf.astype(jnp.float32), norm_gain[2], norm_bias[2], 2
    )
    tran_bf = tran_scaled.astype(jnp.bfloat16)
    hidden_pre = contract("rld,dh->rlh", tran_bf, up_weight)
    hidden_sig = jax.nn.sigmoid(hidden_pre)
    hidden_bf = (hidden_pre * hidden_sig).astype(jnp.bfloat16)
    grad_down = contract("rlh,rld->hd", hidden_bf, cot_rows)
    hidden_grad_bf = (
        contract("rld,hd->rlh", cot_rows, down_weight)
        * hidden_sig
        * (1.0 + hidden_pre * (1.0 - hidden_sig))
    ).astype(jnp.bfloat16)
    grad_up = contract("rld,rlh->dh", tran_bf, hidden_grad_bf)
    tran_grad = contract("rlh,dh->rld", hidden_grad_bf, up_weight)
    first_grad, gain_tran, bias_tran = norm_backward(
        tran_grad, tran_normed, tran_inv, norm_gain[2], 2, (0, 1)
    )
    first_grad = first_grad + cot_rows.astype(jnp.float32)
    update_grad_bf = (first_grad * gate_sig).astype(jnp.bfloat16)
    gate_grad_bf = (first_grad * update * gate_sig * (1.0 - gate_sig)).astype(jnp.bfloat16)
    grad_out = contract("crj,rjd->cd", prod_norm_bf, update_grad_bf)
    norm_grad = contract("rjd,cd->crj", update_grad_bf, out_weight)
    prod_grad, gain_prod, bias_prod = norm_backward(
        norm_grad, prod_normed, prod_inv, norm_gain[1][:, None, None], 0, (1, 2)
    )
    return (
        prod_grad.astype(jnp.bfloat16),
        first_grad,
        gate_grad_bf,
        grad_out,
        grad_up,
        grad_down,
        gain_prod,
        bias_prod,
        gain_tran,
        bias_tran,
    )


def leave_rows(
    left_grad,
    right_grad,
    factor_pre,
    keep_both,
    gate_grad_bf,
    input_bf,
    normed_in,
    inv_in,
    first_grad,
    proj_weight,
    norm_gain,
):
    channels = gate_grad_bf.shape[2]
    sig_left = jax.nn.sigmoid(factor_pre[:channels])
    lin_left = factor_pre[channels : 2 * channels]
    sig_right = jax.nn.sigmoid(factor_pre[2 * channels : 3 * channels])
    lin_right = factor_pre[3 * channels :]
    masked_left = left_grad.astype(jnp.float32) * keep_both
    masked_right = right_grad.astype(jnp.float32) * keep_both
    factor_grad = jnp.concatenate(
        [
            masked_left * lin_left * sig_left * (1.0 - sig_left),
            masked_left * sig_left,
            masked_right * lin_right * sig_right * (1.0 - sig_right),
            masked_right * sig_right,
        ],
        axis=0,
    ).astype(jnp.bfloat16)
    grad_proj = jnp.concatenate(
        [
            contract("rld,erl->de", input_bf, factor_grad),
            contract("rld,rle->de", input_bf, gate_grad_bf),
        ],
        axis=1,
    )
    input_grad = contract("erl,de->rld", factor_grad, proj_weight[:, : 4 * channels]) + contract(
        "rle,de->rld", gate_grad_bf, proj_weight[:, 4 * channels :]
    )
    pair_grad, gain_in, bias_in = norm_backward(
        input_grad, normed_in, inv_in, norm_gain[0], 2, (0, 1)
    )
    return ((pair_grad + first_grad).astype(jnp.bfloat16), grad_proj, gain_in, bias_in)


def channel_products(left_part, right_part):
    return contract("acik,acjk->acij", left_part, right_part).astype(jnp.bfloat16)


def channel_grads(grad_part, left_part, right_part):
    left_grad = contract("acij,acjk->acik", grad_part, right_part).astype(jnp.bfloat16)
    right_grad = contract("acij,acik->acjk", grad_part, left_part).astype(jnp.bfloat16)
    return (left_grad, right_grad)


def channel_plan(
    pair, cotangent, lengths, proj_weight, out_weight, up_weight, down_weight, norm_gain, norm_bias
):
    pair_rows = pair[0]
    cot_rows = cotangent[0]
    rows_here, length_all, channels = pair_rows.shape
    groups = lax.axis_size("row")
    per_group = channels // groups
    first_row = lax.axis_index("row") * rows_here
    row_keep = (first_row + jnp.arange(rows_here, dtype=jnp.int32) < lengths[0]).astype(jnp.float32)
    col_keep = (jnp.arange(length_all, dtype=jnp.int32) < lengths[0]).astype(jnp.float32)
    entered = enter_rows(pair_rows, row_keep, col_keep, proj_weight, norm_gain, norm_bias)
    input_bf, normed_in, inv_in, factor_pre, gate_pre, keep_both, left_bf, right_bf = entered
    left_split = left_bf.reshape(groups, per_group, rows_here, length_all)
    right_split = right_bf.reshape(groups, per_group, rows_here, length_all)
    left_owned, right_owned = (
        lax.all_to_all(left_split, "row", split_axis=0, concat_axis=2, tiled=True),
        lax.all_to_all(right_split, "row", split_axis=0, concat_axis=2, tiled=True),
    )
    product_owned = channel_products(left_owned, right_owned)
    product_split = lax.all_to_all(product_owned, "row", split_axis=2, concat_axis=0, tiled=True)
    product_bf = product_split.reshape(channels, rows_here, length_all)
    middle = middle_rows(
        pair_rows,
        cot_rows,
        product_bf,
        gate_pre,
        out_weight,
        up_weight,
        down_weight,
        norm_gain,
        norm_bias,
    )
    (
        prod_grad_bf,
        first_grad,
        gate_grad_bf,
        grad_out,
        grad_up,
        grad_down,
        gain_prod,
        bias_prod,
        gain_tran,
        bias_tran,
    ) = middle
    grad_split = prod_grad_bf.reshape(groups, per_group, rows_here, length_all)
    grad_owned = lax.all_to_all(grad_split, "row", split_axis=0, concat_axis=2, tiled=True)
    left_home, right_home = lax.all_to_all(
        for_sending(channel_grads(grad_owned, left_owned, right_owned)),
        "row",
        split_axis=2,
        concat_axis=0,
        tiled=True,
    )
    left_grad = left_home.reshape(channels, rows_here, length_all)
    right_grad = right_home.reshape(channels, rows_here, length_all)
    pair_grad, grad_proj, gain_in, bias_in = leave_rows(
        left_grad,
        right_grad,
        factor_pre,
        keep_both,
        gate_grad_bf,
        input_bf,
        normed_in,
        inv_in,
        first_grad,
        proj_weight,
        norm_gain,
    )
    gain_all = jnp.stack([gain_in, gain_prod, gain_tran])
    bias_all = jnp.stack([bias_in, bias_prod, bias_tran])
    summed_proj, summed_out, summed_up, summed_down, summed_gain, summed_bias = lax.psum(
        (grad_proj, grad_out, grad_up, grad_down, gain_all, bias_all), ("crop", "row")
    )
    factor = 1.0 / (rows_here * groups)
    return (
        pair_grad[None],
        summed_proj * factor,
        summed_out * factor,
        summed_up * factor,
        summed_down * factor,
        summed_gain * factor,
        summed_bias * factor,
    )


LANES = 128
SUBLANES = 8
BLOCK_BUDGET = 40 * 1024 * 1024


def dot(lhs, rhs, lhs_dim, rhs_dim):
    return lax.dot_general(
        lhs, rhs, (((lhs_dim,), (rhs_dim,)), ((), ())), preferred_element_type=jnp.float32
    )


def sigmoid(x):
    return 0.5 * jnp.tanh(0.5 * x) + 0.5


def row_mean(x):
    return jnp.mean(x, axis=1, keepdims=True)


def fold(x):
    return jnp.sum(x.reshape(x.shape[0] // SUBLANES, SUBLANES, x.shape[1]), axis=0)


def spread(ref, row):
    return jnp.broadcast_to(ref[pl.ds(row, 1), :], (SUBLANES, LANES))


def norm_back(upstream, normed, inv_std, gain_vec):
    scaled = upstream * gain_vec
    return inv_std * (scaled - row_mean(scaled) - normed * row_mean(scaled * normed))


def block_kernel(
    lines,
    length_all,
    half_rows,
    place_ref,
    own_ref,
    cot_ref,
    near_ref,
    *refs,
):
    line_refs = refs[: lines - 1]
    (
        proj_ref,
        out_ref,
        up_ref,
        down_ref,
        gain_ref,
        bias_ref,
        sum_own_ref,
        sum_near_ref,
    ) = refs[lines - 1 : lines + 7]
    sum_line_refs = refs[lines + 7 : 2 * lines + 6]
    keep_ref, send_ref = refs[2 * lines + 6 : 2 * lines + 8]
    (
        left,
        right,
        left_lin,
        left_sig,
        right_lin,
        right_sig,
        scaled_in,
        normed_in,
        inv_in,
        product,
        prod_grad,
        prod_turned,
        left_grad,
        right_grad,
        gate_back,
        first_back,
        terms,
    ) = refs[2 * lines + 8 :]
    rows = own_ref.shape[0]
    per = SUBLANES * SUBLANES
    mid_rows = lines * per
    channels = LANES
    hidden_units = up_ref.shape[1]
    count = place_ref[0]
    me = place_ref[1]
    core = place_ref[2]
    step = 256
    zero_tile = jnp.zeros((SUBLANES, LANES), jnp.float32)

    def vec(ref, n):
        return ref[n : n + 1, :]

    def enter(values, slot, owner, left_slot, right_slot):
        for start in range(0, rows, step):
            span = pl.ds(start, step)
            x = values(span).astype(jnp.float32)
            center = x - row_mean(x)
            inv_std = lax.rsqrt(row_mean(center * center) + EPSILON)
            normed = center * inv_std
            scaled = (normed * vec(gain_ref, 0) + vec(bias_ref, 0)).astype(jnp.bfloat16)
            normed_in[slot, span, :] = normed
            inv_in[slot, span, :] = jnp.broadcast_to(inv_std, normed.shape)
            scaled_in[slot, span, :] = scaled
            at = lax.broadcasted_iota(jnp.int32, (step, LANES), 0) + start
            kept = (at // SUBLANES < count) & (at % SUBLANES + owner * SUBLANES < count)
            keep = kept.astype(jnp.float32)
            for target, lin, sig, pick, offset in (
                (left, left_lin, left_sig, left_slot, 0),
                (right, right_lin, right_sig, right_slot, 2 * channels),
            ):
                if pick is None:
                    continue
                pre = dot(scaled, proj_ref[:, offset : offset + 2 * channels], 1, 0)
                sig_pre = sigmoid(pre[:, :channels])
                kept_sig = sig_pre * keep
                value = kept_sig * pre[:, channels:]
                where = pl.ds(pick * rows + start, step)
                target[where, :] = value.astype(jnp.bfloat16).astype(jnp.float32)
                lin[where, :] = value * (1.0 - sig_pre)
                sig[where, :] = kept_sig

    enter(lambda span: own_ref[span, :], 0, me, 0, 0)
    enter(lambda span: near_ref[0, span, :], lines, me ^ 1, 1, None)
    for q in range(1, lines):
        enter(lambda span, q=q: line_refs[q - 1][span, :], q, me ^ (2 * q), None, q)

    def product_of(q, carry):
        acc = [zero_tile] * (2 * SUBLANES)
        for k in range(length_all):
            sides = [left[pl.ds(b * rows + k * SUBLANES, SUBLANES), :] for b in range(2)]
            for j in range(SUBLANES):
                other = spread(right, q * rows + k * SUBLANES + j)
                for b in range(2):
                    acc[b * SUBLANES + j] = acc[b * SUBLANES + j] + sides[b] * other
        for b in range(2):
            for j in range(SUBLANES):
                base = pl.multiple_of(b * mid_rows + q * per + j * SUBLANES, SUBLANES)
                product[pl.ds(base, SUBLANES), :] = acc[b * SUBLANES + j]
        return carry

    lax.fori_loop(0, lines, product_of, 0)

    gate_back[...] = jnp.zeros(gate_back.shape, jnp.float32)
    first_back[...] = jnp.zeros(first_back.shape, jnp.float32)
    out_term = jnp.zeros((channels, channels), jnp.float32)
    gate_term = jnp.zeros((channels, channels), jnp.float32)
    up_term = jnp.zeros((channels, hidden_units), jnp.float32)
    down_term = jnp.zeros((channels, hidden_units), jnp.float32)
    gain_prod = bias_prod = gain_tran = bias_tran = zero_tile
    spots = [pl.multiple_of((me ^ (2 * q)) * per, per) for q in range(lines)]

    for b in range(2):
        slot = lines if b else 0

        def pick(read):
            return jnp.concatenate([read(pl.ds(spot, per)) for spot in spots], axis=0)

        if b:
            pair_rows = pick(lambda span: near_ref[0, span, :])
            cot_rows = pick(lambda span: near_ref[1, span, :])
        else:
            pair_rows = pick(lambda span: own_ref[span, :])
            cot_rows = pick(lambda span: cot_ref[span, :])
        scaled_rows = pick(lambda span: scaled_in[slot, span, :])
        prod = product[b * mid_rows : (b + 1) * mid_rows, :]
        prod = prod.astype(jnp.bfloat16).astype(jnp.float32)
        prod_normed, prod_inv, prod_scaled = norm_forward(
            prod, vec(gain_ref, 1), vec(bias_ref, 1), 1
        )
        prod_norm_bf = prod_scaled.astype(jnp.bfloat16)
        update = dot(prod_norm_bf, out_ref[...], 1, 0)
        gate_sig = sigmoid(dot(scaled_rows, proj_ref[:, 4 * channels :], 1, 0))
        first_bf = (pair_rows.astype(jnp.float32) + gate_sig * update).astype(jnp.bfloat16)
        tran_normed, tran_inv, tran_scaled = norm_forward(
            first_bf.astype(jnp.float32), vec(gain_ref, 2), vec(bias_ref, 2), 1
        )
        tran_bf = tran_scaled.astype(jnp.bfloat16)
        hidden_pre = dot(tran_bf, up_ref[...], 1, 0)
        hidden_sig = sigmoid(hidden_pre)
        hidden_bf = (hidden_pre * hidden_sig).astype(jnp.bfloat16)
        down_term = down_term + dot(cot_rows, hidden_bf, 0, 0)
        hidden_grad_bf = (
            dot(cot_rows, down_ref[...], 1, 1)
            * hidden_sig
            * (1.0 + hidden_pre * (1.0 - hidden_sig))
        ).astype(jnp.bfloat16)
        up_term = up_term + dot(tran_bf, hidden_grad_bf, 0, 0)
        tran_grad = dot(hidden_grad_bf, up_ref[...], 1, 1)
        gain_tran = gain_tran + fold(tran_grad * tran_normed)
        bias_tran = bias_tran + fold(tran_grad)
        first_grad = cot_rows.astype(jnp.float32) + norm_back(
            tran_grad, tran_normed, tran_inv, vec(gain_ref, 2)
        )
        gated = first_grad * gate_sig
        update_grad_bf = gated.astype(jnp.bfloat16)
        gate_grad_bf = (gated * update * (1.0 - gate_sig)).astype(jnp.bfloat16)
        out_term = out_term + dot(prod_norm_bf, update_grad_bf, 0, 0)
        gate_term = gate_term + dot(scaled_rows, gate_grad_bf, 0, 0)
        norm_grad = dot(update_grad_bf, out_ref[...], 1, 1)
        gain_prod = gain_prod + fold(norm_grad * prod_normed)
        bias_prod = bias_prod + fold(norm_grad)
        back = norm_back(norm_grad, prod_normed, prod_inv, vec(gain_ref, 1))
        prod_grad[b * mid_rows : (b + 1) * mid_rows, :] = back.astype(jnp.bfloat16).astype(
            jnp.float32
        )
        gate_input = dot(gate_grad_bf, proj_ref[:, 4 * channels :], 1, 1)
        for q in range(lines):
            span = pl.ds(spots[q], per)
            gate_back[b, span, :] = gate_input[q * per : (q + 1) * per, :]
            first_back[b, span, :] = first_grad[q * per : (q + 1) * per, :]

    for b in range(2):
        for i in range(SUBLANES):
            for q in range(lines):
                prod_turned[
                    (b * SUBLANES + i) * lines * SUBLANES + q * SUBLANES : (b * SUBLANES + i)
                    * lines
                    * SUBLANES
                    + (q + 1) * SUBLANES,
                    :,
                ] = prod_grad[pl.ds(b * mid_rows + q * per + i, SUBLANES, stride=SUBLANES), :]

    def left_of(group, carry):
        first = group * SUBLANES
        acc = [zero_tile] * (2 * SUBLANES)
        for q in range(lines):
            for j in range(SUBLANES):
                base = q * per + j * SUBLANES
                sides = [prod_grad[b * mid_rows + base : b * mid_rows + base + SUBLANES, :] for b in range(2)]
                for k in range(SUBLANES):
                    other = spread(right, q * rows + (first + k) * SUBLANES + j)
                    for b in range(2):
                        acc[b * SUBLANES + k] = acc[b * SUBLANES + k] + sides[b] * other
        for b in range(2):
            for k in range(SUBLANES):
                base = pl.multiple_of(b * rows + (first + k) * SUBLANES, SUBLANES)
                left_grad[pl.ds(base, SUBLANES), :] = acc[b * SUBLANES + k]
        return carry

    lax.fori_loop(0, length_all // SUBLANES, left_of, 0)

    batch = 4

    def right_of(group, carry):
        first = group * batch
        acc = [zero_tile] * (lines * batch)
        for b in range(2):
            for i in range(SUBLANES):
                base = (b * SUBLANES + i) * lines * SUBLANES
                sides = [
                    prod_turned[base + q * SUBLANES : base + (q + 1) * SUBLANES, :]
                    for q in range(lines)
                ]
                for k in range(batch):
                    other = spread(left, b * rows + (first + k) * SUBLANES + i)
                    for q in range(lines):
                        acc[q * batch + k] = acc[q * batch + k] + sides[q] * other
        for q in range(lines):
            for k in range(batch):
                base = pl.multiple_of(q * rows + (first + k) * SUBLANES, SUBLANES)
                right_grad[pl.ds(base, SUBLANES), :] = acc[q * batch + k]
        return carry

    lax.fori_loop(0, length_all // batch, right_of, 0)

    left_term = jnp.zeros((channels, 2 * channels), jnp.float32)
    right_term = jnp.zeros((channels, 2 * channels), jnp.float32)
    gain_in = bias_in = zero_tile

    def factor(grad, lin, sig, pick, start):
        where = pl.ds(pick * rows + start, step)
        values = grad[where, :]
        return jnp.concatenate(
            [(values * lin[where, :]).astype(jnp.bfloat16), (values * sig[where, :]).astype(jnp.bfloat16)],
            axis=1,
        )

    for slot in range(lines + 1):
        left_slot = 0 if slot == 0 else (1 if slot == lines else None)
        right_slot = slot if slot < lines else None
        for start in range(0, rows, step):
            span = pl.ds(start, step)
            scaled = scaled_in[slot, span, :]
            normed = normed_in[slot, span, :]
            upstream = None
            if left_slot is not None:
                part = factor(left_grad, left_lin, left_sig, left_slot, start)
                left_term = left_term + dot(scaled, part, 0, 0)
                upstream = dot(part, proj_ref[:, : 2 * channels], 1, 1) + gate_back[left_slot, span, :]
            if right_slot is not None:
                part = factor(right_grad, right_lin, right_sig, right_slot, start)
                right_term = right_term + dot(scaled, part, 0, 0)
                more = dot(part, proj_ref[:, 2 * channels : 4 * channels], 1, 1)
                upstream = more if upstream is None else upstream + more
            gain_in = gain_in + fold(upstream * normed)
            bias_in = bias_in + fold(upstream)
            total = norm_back(upstream, normed, inv_in[slot, span, :], vec(gain_ref, 0))
            if left_slot is not None:
                total = total + first_back[left_slot, span, :]
            if slot == 0:
                sum_own_ref[span, :] = total
            elif slot == lines:
                sum_near_ref[span, :] = total.astype(jnp.bfloat16)
            else:
                sum_line_refs[slot - 1][span, :] = total.astype(jnp.bfloat16)

    at = 0
    for block in range(hidden_units // LANES):
        terms[at : at + LANES, :] = down_term[:, block * LANES : (block + 1) * LANES].T
        at += LANES
    for whole in (up_term, out_term, left_term, right_term, gate_term):
        for block in range(whole.shape[1] // LANES):
            terms[at : at + LANES, :] = whole[:, block * LANES : (block + 1) * LANES]
            at += LANES
    sums = [
        jnp.sum(value, axis=0, keepdims=True)
        for value in (gain_in, gain_prod, gain_tran, bias_in, bias_prod, bias_tran)
    ]
    terms[at:, :] = jnp.zeros((2 * half_rows - at, LANES), jnp.float32)
    for n, value in enumerate(sums):
        terms[at + n : at + n + 1, :] = value
    keep_ref[...] = terms[pl.ds(pl.multiple_of(core * half_rows, SUBLANES), half_rows), :]
    send_ref[...] = terms[
        pl.ds(pl.multiple_of((1 - core) * half_rows, SUBLANES), half_rows), :
    ].astype(jnp.bfloat16)


def xor_pairs(count, mask):
    return [(n, n ^ mask) for n in range(count)]


def block_plan(
    pair, cotangent, lengths, proj_weight, out_weight, up_weight, down_weight, norm_gain, norm_bias
):
    _, rows_here, length_all, channels = pair.shape
    hidden_units = up_weight.shape[1]
    groups = lax.axis_size("row")
    crops = lax.axis_size("crop")
    lines = groups // 2
    me = lax.axis_index("row")
    crop = lax.axis_index("crop")
    core = crop & 1
    rows = rows_here * length_all

    def turned(values):
        return jnp.swapaxes(values[0], 0, 1).reshape(rows, channels)

    pair_turned = turned(pair)
    cot_turned = turned(cotangent)
    line_blocks = [
        lax.ppermute(pair_turned, "row", xor_pairs(groups, 2 * q)) for q in range(1, lines)
    ]
    near = lax.ppermute(jnp.stack([pair_turned, cot_turned]), "row", xor_pairs(groups, 1))
    place = jnp.stack([lengths[0], me, core]).astype(jnp.int32)

    used_rows = channels * (
        (2 * hidden_units + channels + proj_weight.shape[1]) // LANES
    ) + 6
    unit = 4 * 2 * SUBLANES
    half_rows = -(-used_rows // (2 * unit)) * unit

    f32 = jnp.float32
    vmem = pl.BlockSpec(memory_space=pltpu.VMEM)
    block_bf = jax.ShapeDtypeStruct((rows, channels), jnp.bfloat16)
    mid = 2 * lines * SUBLANES * SUBLANES
    outs = pl.pallas_call(
        functools.partial(block_kernel, lines, length_all, half_rows),
        out_shape=[jax.ShapeDtypeStruct((rows, channels), f32)]
        + [block_bf] * lines
        + [
            jax.ShapeDtypeStruct((half_rows, LANES), f32),
            jax.ShapeDtypeStruct((half_rows, LANES), jnp.bfloat16),
        ],
        in_specs=[pl.BlockSpec(memory_space=pltpu.SMEM)] + [vmem] * (lines + 8),
        out_specs=[vmem] * (lines + 3),
        scratch_shapes=[
            pltpu.VMEM((2 * rows, LANES), f32),
            pltpu.VMEM((lines * rows, LANES), f32),
            pltpu.VMEM((2 * rows, LANES), f32),
            pltpu.VMEM((2 * rows, LANES), f32),
            pltpu.VMEM((lines * rows, LANES), f32),
            pltpu.VMEM((lines * rows, LANES), f32),
            pltpu.VMEM((lines + 1, rows, LANES), jnp.bfloat16),
            pltpu.VMEM((lines + 1, rows, LANES), f32),
            pltpu.VMEM((lines + 1, rows, LANES), f32),
            pltpu.VMEM((mid, LANES), f32),
            pltpu.VMEM((mid, LANES), f32),
            pltpu.VMEM((mid, LANES), f32),
            pltpu.VMEM((2 * rows, LANES), f32),
            pltpu.VMEM((lines * rows, LANES), f32),
            pltpu.VMEM((2, rows, LANES), f32),
            pltpu.VMEM((2, rows, LANES), f32),
            pltpu.VMEM((2 * half_rows, LANES), f32),
        ],
        name="block_kernel",
    )(
        place,
        pair_turned,
        cot_turned,
        near,
        *line_blocks,
        proj_weight,
        out_weight,
        up_weight,
        down_weight,
        norm_gain,
        norm_bias,
    )
    sum_own, sum_near, sum_lines = outs[0], outs[1], outs[2 : lines + 1]
    keep, send = outs[lines + 1 :]

    home = [lax.ppermute(sum_near, "row", xor_pairs(groups, 1))] + [
        lax.ppermute(part, "row", xor_pairs(groups, 2 * (q + 1)))
        for q, part in enumerate(sum_lines)
    ]
    half = keep + lax.ppermute(send, "crop", xor_pairs(crops, 1)).astype(f32)

    both = ("crop", "row")
    total = crops * groups
    quarter = half_rows // 4
    mine = (crop >> 1) * 2 + (me & 1)

    def flat_pairs(mask):
        return [
            (n, n ^ ((mask >> 1) * 2 * groups + (mask & 1))) for n in range(total)
        ]

    quarters = half.reshape(4, quarter, LANES)

    def quarter_of(n):
        return lax.dynamic_index_in_dim(quarters, n, 0, keepdims=False)

    summed = quarter_of(mine)
    for mask in (1, 2, 3):
        part = quarter_of(mine ^ mask).astype(jnp.bfloat16)
        summed = summed + lax.ppermute(part, both, flat_pairs(mask)).astype(f32)
    rounded = summed.astype(jnp.bfloat16)
    parts = [rounded] + [
        lax.ppermute(rounded, "row", xor_pairs(groups, 2 * q)) for q in range(1, lines)
    ]
    parts = [part.astype(f32) for part in parts]
    while len(parts) > 1:
        parts = [parts[n] + parts[n + 1] for n in range(0, len(parts), 2)]
    rounded = parts[0].astype(jnp.bfloat16)
    other = lax.ppermute(rounded, "crop", xor_pairs(crops, 1))
    pieces = jnp.stack([rounded, other])
    gathered = [pieces] + [lax.ppermute(pieces, both, flat_pairs(mask)) for mask in (1, 2, 3)]
    stacked = jnp.stack(gathered)
    ordered = jnp.stack(
        [
            jnp.stack(
                [
                    lax.dynamic_index_in_dim(
                        lax.dynamic_index_in_dim(stacked, mine ^ n, 0, keepdims=False),
                        core ^ c,
                        0,
                        keepdims=False,
                    )
                    for n in range(4)
                ]
            )
            for c in range(2)
        ]
    )
    flat = ordered.reshape(2 * half_rows, LANES).astype(f32) * (1.0 / (rows_here * groups))
    at = hidden_units
    result_down = flat[:at]

    def take(columns):
        nonlocal at
        count = columns // LANES
        value = flat[at : at + count * channels].reshape(count, channels, LANES)
        at += count * channels
        return jnp.swapaxes(value, 0, 1).reshape(channels, columns)

    result_up = take(hidden_units)
    result_out = take(channels)
    result_proj = take(proj_weight.shape[1])
    result_gain = flat[at : at + 3]
    result_bias = flat[at + 3 : at + 6]
    grad = sum_own
    for part in home:
        grad = grad + part.astype(f32)
    grad = jnp.swapaxes(grad.astype(jnp.bfloat16).reshape(length_all, rows_here, channels), 0, 1)
    return (
        grad[None],
        result_proj,
        result_out,
        result_up,
        result_down,
        result_gain,
        result_bias,
    )


def power_of_two(n):
    return n & (n - 1) == 0


def local(
    pair, cotangent, lengths, proj_weight, out_weight, up_weight, down_weight, norm_gain, norm_bias
):
    _, rows_here, length_all, channels = pair.shape
    groups = lax.axis_size("row")
    crops = lax.axis_size("crop")
    held = (groups // 2 + 2) * 6 * 4 * rows_here * length_all * channels
    fits = (
        rows_here == SUBLANES
        and channels == LANES
        and length_all % SUBLANES == 0
        and groups >= 4
        and crops == 4
        and power_of_two(groups)
        and held <= BLOCK_BUDGET
    )
    plan = block_plan if fits else channel_plan
    return plan(
        pair,
        cotangent,
        lengths,
        proj_weight,
        out_weight,
        up_weight,
        down_weight,
        norm_gain,
        norm_bias,
    )


def solution(mesh):
    in_specs = (
        P("crop", "row", None, None),
        P("crop", "row", None, None),
        P("crop"),
        P(),
        P(),
        P(),
        P(),
        P(),
        P(),
    )
    out_specs = (P("crop", "row", None, None), P(), P(), P(), P(), P(), P())
    return jax.shard_map(local, mesh=mesh, in_specs=in_specs, out_specs=out_specs, check_vma=False)
```
